256 devices in a mesh: feed: 128 (over z_lo, x, y, core), tm: 2 (over z_hi).
Axes of the slice: x: 4, y: 4, z: 8 (z_hi: 2, z_lo: 4; z = z_hi * 4 + z_lo), core: 2. Of those that a mesh axis runs over, the one named last changes fastest.
Arguments:
- samples: bfloat16 [2048, 12288], P('feed', 'tm'), may hold values from -6 to 6
- filter_taps: float32 [4, 1024], replicated, may hold values from -3 to 3
- feed_cylinder: int32 [2048], replicated, may hold values from 0 to 3
- feed_delay: int32 [2048], replicated, may hold values from 0 to 4095
- pointing: int32 [512, 4], replicated, may hold values from 0 to 4095
- chirp_rate: float32 [512], P('feed'), may hold values from 1 to 40
Outputs:
- series: float32 [512, 12, 1024], P('feed', 'tm')
The draws below stay inside these ranges and needn't reach their ends.
All inputs are finite; a program needn't handle non-finite values.
Results may differ from the reference program's by a relative error of at most 0.0046.
Values may be sent and summed in bfloat16 or wider, within the bound.
A program may use at most 64 MiB of HBM per device.

```python
import math
import jax
import jax.numpy as jnp
from jax import lax

FEEDS = 2048
NCHAN = 512
BEAMS = 512
TAPS = 4
CYL = 4
PHASES = 4096
FRAMES = 12


def place_ends(entries, rng, smallest, high):
    longest = entries.shape.index(max(entries.shape))
    spots = []
    for shift in (0, 1):
        where = [jax.random.randint(jax.random.fold_in(rng, axis), (), 0, length) for axis, length in enumerate(entries.shape)]
        where[longest] = (where[longest] + shift) % entries.shape[longest]
        spots.append(tuple(where))
    return entries.at[spots[0]].set(smallest).at[spots[1]].set(high)


def steps_of(own_key, shape, pieces, smallest, top_value):
    gain, own = 1.0, jax.random.fold_in(own_key, 6)
    for dim, blocks in pieces:
        heights = jnp.exp(jax.random.uniform(jax.random.fold_in(own, dim), (blocks,), jnp.float32, smallest / len(pieces), top_value / len(pieces)))
        gain = gain * jnp.repeat(heights, shape[dim] // blocks).reshape([-1 if axis == dim else 1 for axis in range(len(shape))])
    return gain


def noise(own_key, extent, deviation, reach, shards=(), kind=jnp.bfloat16):
    entries = jax.random.normal(own_key, extent, jnp.float32) * deviation
    if len(shards) > 0:
        entries = steps_of(own_key, extent, shards, -0.22, 0.18) * entries
    return jnp.clip(entries, min=-reach, max=reach).astype(kind)


def setup_inputs(seed: int = 0) -> dict:
    splits = jax.random.split(jax.random.key(seed), 7)
    samples = noise(splits[0], (FEEDS, FRAMES * 2 * NCHAN), 1.0, 6.0, ((0, 128), (1, 2)))
    filter_taps = noise(splits[1], (TAPS, 2 * NCHAN), 0.5, 3.0, (), jnp.float32)
    feed_cylinder = place_ends(jax.random.randint(splits[2], (FEEDS,), 0, CYL), jax.random.fold_in(splits[2], 1), 0, CYL - 1).astype(jnp.int32)
    feed_delay = place_ends(jax.random.randint(splits[3], (FEEDS,), 0, PHASES), jax.random.fold_in(splits[3], 1), 0, PHASES - 1).astype(jnp.int32)
    pointing = place_ends(jax.random.randint(splits[4], (BEAMS, CYL), 0, PHASES), jax.random.fold_in(splits[4], 1), 0, PHASES - 1).astype(jnp.int32)
    chirp_rate = jnp.clip(jnp.exp(math.log(40.0) - 3.6888795 * jax.random.uniform(splits[5], (BEAMS,), jnp.float32) ** steps_of(splits[5], (BEAMS,), ((0, 128),), -0.2, 0.2)), 1.0, 40.0)
    return {"samples": samples, "filter_taps": filter_taps, "feed_cylinder": feed_cylinder, "feed_delay": feed_delay, "pointing": pointing, "chirp_rate": chirp_rate}


def reference(samples, filter_taps, feed_cylinder, feed_delay, pointing, chirp_rate):
    length = 2 * NCHAN
    frames = samples.astype(jnp.float32).reshape(FEEDS, FRAMES, length)
    padded = jnp.concatenate([jnp.zeros((FEEDS, TAPS - 1, length), jnp.float32), frames], axis=1)
    filtered = jnp.zeros((FEEDS, FRAMES, length), jnp.float32)
    for tap_index in range(TAPS):
        filtered = filtered + filter_taps[tap_index] * padded[:, tap_index:tap_index + FRAMES, :]
    spectrum = jnp.fft.rfft(filtered, axis=-1)[..., :NCHAN]
    norm_forward = 1.0 / math.sqrt(length)
    spec_real = (jnp.real(spectrum) * norm_forward).astype(jnp.bfloat16)
    spec_imag = (jnp.imag(spectrum) * norm_forward).astype(jnp.bfloat16)
    chan_real = jnp.transpose(spec_real, (2, 1, 0)).reshape(NCHAN // 8, 8, FRAMES, FEEDS)
    chan_imag = jnp.transpose(spec_imag, (2, 1, 0)).reshape(NCHAN // 8, 8, FRAMES, FEEDS)
    steer = jnp.transpose(pointing[:, feed_cylinder])
    channel_ids = jnp.arange(NCHAN, dtype=jnp.int32).reshape(NCHAN // 8, 8)
    beam_scale = 1.0 / math.sqrt(FEEDS)

    def beam_block(inputs):
        local_real, local_imag, ids = inputs
        turns = (ids[:, None] + 1) * feed_delay[None, :] % PHASES
        phase = turns[:, :, None] * steer[None, :, :] % PHASES
        angle = phase.astype(jnp.float32) * (2.0 * math.pi / PHASES)
        w_real = jnp.cos(angle).astype(jnp.bfloat16).astype(jnp.float32)
        w_imag = jnp.sin(angle).astype(jnp.bfloat16).astype(jnp.float32)
        x_real = local_real.astype(jnp.float32)
        x_imag = local_imag.astype(jnp.float32)
        beam_real = jnp.einsum('cfj,cjb->cfb', x_real, w_real) - jnp.einsum('cfj,cjb->cfb', x_imag, w_imag)
        beam_imag = jnp.einsum('cfj,cjb->cfb', x_real, w_imag) + jnp.einsum('cfj,cjb->cfb', x_imag, w_real)
        return ((beam_real * beam_scale).astype(jnp.bfloat16), (beam_imag * beam_scale).astype(jnp.bfloat16))
    beams_real, beams_imag = lax.map(beam_block, (chan_real, chan_imag, channel_ids))
    beams_real = beams_real.reshape(NCHAN, FRAMES, BEAMS).astype(jnp.float32)
    beams_imag = beams_imag.reshape(NCHAN, FRAMES, BEAMS).astype(jnp.float32)
    position = jnp.arange(NCHAN).astype(jnp.float32) / NCHAN
    chirp = (jnp.pi * chirp_rate)[None, :] * (position * position)[:, None]
    chirp_cos = jnp.cos(chirp)[:, None, :]
    chirp_sin = jnp.sin(chirp)[:, None, :]
    chirped_real = beams_real * chirp_cos - beams_imag * chirp_sin
    chirped_imag = beams_real * chirp_sin + beams_imag * chirp_cos
    chirped = jnp.transpose(chirped_real + 1j * chirped_imag, (2, 1, 0))
    synthesized = jnp.fft.ifft(chirped, axis=-1) * math.sqrt(NCHAN)
    return jnp.concatenate([jnp.real(synthesized), jnp.imag(synthesized)], axis=-1).astype(jnp.float32)
```

```python
import math

import jax
import jax.numpy as jnp
import numpy as np
from jax import lax
from jax.experimental import pallas as pl
from jax.experimental.pallas import tpu as pltpu
from jax.sharding import PartitionSpec as P

FEEDS = 2048
NCHAN = 512
BEAMS = 512
TAPS = 4
CYL = 4
PHASES = 4096
GROUPS = 128
NDEV = 256
MESH = pl.DeviceIdType.MESH
BF = jnp.bfloat16
F32 = jnp.float32
VMEM = pl.BlockSpec(memory_space=pltpu.VMEM)

def _fit():
    grid = np.cos(np.pi * (np.arange(4000) + 0.5) / 8000) * 0.5
    sq = grid * grid
    sine = np.sin(np.pi * grid) / grid * math.sqrt(2.0)
    cosine = np.cos(np.pi * grid) * math.sqrt(2.0)
    mat = np.stack([sq**k for k in range(5)], axis=1)
    s = np.linalg.lstsq(mat * grid[:, None], sine * grid, rcond=None)[0]
    c = np.linalg.lstsq(mat, cosine, rcond=None)[0]
    return [float(v) for v in s], [float(v) for v in c]


SIN_C, COS_C = _fit()
ROUND = 1.5 * 2.0**23


def cos_sin(turns):
    r = turns - ((turns + ROUND) - ROUND)
    q = r * r
    s = SIN_C[4]
    c = COS_C[4]
    for k in (3, 2, 1, 0):
        s = s * q + SIN_C[k]
        c = c * q + COS_C[k]
    s = s * r
    return 1.0 - s * s, s * c


def split_const(x):
    hi = x.astype(np.float32).astype(BF)
    lo = (x - hi.astype(np.float64)).astype(np.float32).astype(BF)
    return np.stack([hi, lo])


def forward_rows():
    n = np.arange(NCHAN)[None, :]
    out = []
    for par in range(2):
        c = 2 * np.arange(NCHAN // 2)[:, None] + par
        ang = (n * c % (2 * NCHAN)) * (2.0 * np.pi / (2 * NCHAN))
        both = np.stack([np.cos(ang), -np.sin(ang)], axis=1) / math.sqrt(2 * NCHAN)
        out.append(both.reshape(NCHAN, NCHAN))
    return split_const(np.stack(out))


def inverse_rows():
    t = np.arange(NCHAN // 2)[None, :]
    out = []
    for par in range(2):
        c = 2 * np.arange(NCHAN // 2)[:, None] + par
        ang = (t * c % NCHAN) * (2.0 * np.pi / NCHAN)
        out.append(np.concatenate([np.cos(ang), np.sin(ang)], axis=1) / math.sqrt(NCHAN))
    return split_const(np.stack(out))


def split(x):
    hi = x.astype(BF)
    return hi, (x - hi.astype(F32)).astype(BF)


def nt(a, b):
    return lax.dot_general(a, b, (((1,), (1,)), ((), ())), preferred_element_type=F32)


def dft_kernel(x_ref, tail_ref, taps_ref, basis_ref, o_ref, fold):
    length = 2 * NCHAN
    fold[...] = jnp.zeros_like(fold)
    for f in range(6):
        acc = None
        for k in range(TAPS):
            src = f + k - 3
            if src < 0:
                piece = tail_ref[:, (src + 3) * length : (src + 4) * length]
            else:
                piece = x_ref[:, src * length : (src + 1) * length]
            term = taps_ref[k : k + 1, :] * piece.astype(F32)
            acc = term if acc is None else acc + term
        a, b = acc[:, :NCHAN], acc[:, NCHAN:]
        fold[0, f * 16 : f * 16 + 16, :] = a + b
        fold[1, f * 16 : f * 16 + 16, :] = a - b
    for par in range(2):
        hi, lo = split(fold[par])
        top = basis_ref[0, par]
        out = nt(top, hi) + nt(top, lo) + nt(basis_ref[1, par], hi)
        o_ref[par] = out.astype(BF).reshape(NDEV, 2, 128)


def exchange_kernel(strided, x_ref, o_ref, send_sem, recv_sem):
    feed = lax.axis_index("feed")
    tm = lax.axis_index("tm")
    me = tm * GROUPS + feed
    barrier = pltpu.get_barrier_semaphore()

    def place(k):
        return lax.rem(feed + k, GROUPS), lax.rem(tm + (feed + k) // GROUPS, 2)

    def signal(k, carry):
        f, t = place(k)
        pl.semaphore_signal(barrier, inc=1, device_id=(f, t), device_id_type=MESH)
        return carry

    def view(ref, at):
        return ref.at[:, at] if strided else ref.at[at]

    def send(k, carry):
        f, t = place(k)
        pltpu.make_async_remote_copy(
            src_ref=view(x_ref, t * GROUPS + f), dst_ref=view(o_ref, me),
            send_sem=send_sem, recv_sem=recv_sem, device_id=(f, t), device_id_type=MESH,
        ).start()
        return carry

    lax.fori_loop(1, NDEV, signal, 0, unroll=15)
    pl.semaphore_wait(barrier, NDEV - 1)
    lax.fori_loop(1, NDEV, send, 0, unroll=15)
    if strided:
        o_ref[:, me] = x_ref[:, me]
    else:
        o_ref[me] = x_ref[me]
    some = (lambda r: r.at[:, pl.ds(0, NDEV - 1)]) if strided else (lambda r: r.at[pl.ds(0, NDEV - 1)])
    pltpu.make_async_remote_copy(
        src_ref=some(x_ref), dst_ref=some(o_ref), send_sem=send_sem, recv_sem=recv_sem,
        device_id=(feed, tm), device_id_type=MESH,
    ).wait()


def exchange(x, cid):
    import functools
    return pl.pallas_call(
        functools.partial(exchange_kernel, x.ndim == 4),
        out_shape=jax.ShapeDtypeStruct(x.shape, x.dtype),
        in_specs=[VMEM], out_specs=VMEM,
        scratch_shapes=[pltpu.SemaphoreType.DMA, pltpu.SemaphoreType.DMA],
        compiler_params=pltpu.CompilerParams(collective_id=cid, has_side_effects=True),
    )(x)


def beam_kernel(r_ref, delay_ref, cyl_ref, point_ref, o_ref, w_ref, wide, turned, lhs):
    m = lax.axis_index("tm") * GROUPS + lax.axis_index("feed")
    delay = delay_ref[...].astype(F32)
    cyl = cyl_ref[...]
    turns = []
    for par in range(2):
        t = (2 * m + par + 1).astype(F32) * delay
        turns.append(t - jnp.floor(t * (1.0 / PHASES)) * PHASES)
    point = point_ref[...].astype(F32) * (1.0 / PHASES)
    for i in range(16):
        kind = jnp.broadcast_to(cyl[:, i : i + 1], (GROUPS, 128))
        t0 = jnp.broadcast_to(turns[0][:, i : i + 1], (GROUPS, 128))
        t1 = jnp.broadcast_to(turns[1][:, i : i + 1], (GROUPS, 128))
        for lt in range(4):
            lanes = slice(lt * 128, lt * 128 + 128)
            p = point[:, lanes]
            steer = jnp.where(kind == 0, p[0:1], jnp.where(kind == 1, p[1:2], jnp.where(kind == 2, p[2:3], p[3:4])))
            for par, t in ((0, t0), (1, t1)):
                c, s = cos_sin(t * steer)
                w_ref[par, i * 128 : i * 128 + 128, lt * 128 : lt * 128 + 128] = c.astype(BF)
                w_ref[par, i * 128 : i * 128 + 128, 512 + lt * 128 : 512 + lt * 128 + 128] = s.astype(BF)
    for par in range(2):
        wide[...] = r_ref[par].astype(F32).reshape(2 * NDEV, 128)
        for ri in range(2):
            for tm in range(2):
                block = wide[pl.ds(tm * 256 + ri, 128, stride=2), :]
                turned[(ri * 2 + tm) * 128 : (ri * 2 + tm) * 128 + 128, :] = block.T
        for i in range(16):
            lhs[:, i * 128 : i * 128 + 128] = turned[pl.ds(i, 32, stride=16), :].astype(BF)
        prod = jnp.dot(lhs[...], w_ref[par], preferred_element_type=F32)
        scale = 1.0 / math.sqrt(FEEDS)
        real = (prod[:16, :512] - prod[16:, 512:]) * scale
        imag = (prod[:16, 512:] + prod[16:, :512]) * scale
        for tm in range(2):
            o_ref[tm * 32 + par * 16 : tm * 32 + par * 16 + 8, :] = real[tm * 8 : tm * 8 + 8]
            o_ref[tm * 32 + par * 16 + 8 : tm * 32 + par * 16 + 16, :] = imag[tm * 8 : tm * 8 + 8]


def pack_kernel(b_ref, o_ref, flip, wide):
    flip[...] = jnp.zeros_like(flip)
    for q in range(4):
        block = jnp.concatenate([b_ref[:, q * 128 : q * 128 + 128], jnp.zeros((64, 128), F32)], axis=0)
        flip[q * 128 : q * 128 + 128, :] = block.T
    wide[...] = jnp.zeros_like(wide)
    for tm in range(2):
        acc = None
        lane = lax.broadcasted_iota(jnp.int32, (128, 128), 1) // 32
        for b in range(4):
            rows = flip[pl.ds(b, 128, stride=4), :]
            moved = pltpu.roll(rows, (32 * (b - tm)) % 128, 1)
            acc = moved if acc is None else jnp.where(lane == b, moved, acc)
        wide[pl.ds(tm * 256, 128, stride=2), :] = acc
    o_ref[...] = wide[...].astype(BF).reshape(NDEV, 2, 128)


def synth_kernel(q_ref, rate_ref, basis_ref, o_ref, wide, turned):
    wide[...] = q_ref[...].astype(F32).reshape(2 * NDEV, 128)
    for h in range(2):
        turned[:, h * 128 : h * 128 + 128] = wide[pl.ds(h * 256, 128, stride=2), :].T
    s = lax.broadcasted_iota(jnp.int32, (8, 256), 1)
    halves = []
    for par in range(2):
        pos = (2 * s + par).astype(F32) * (1.0 / NCHAN)
        real, imag = [], []
        for b in range(4):
            c, sn = cos_sin((0.5 * rate_ref[b]) * (pos * pos))
            at = b * 32 + par * 16
            xr = turned[at : at + 8, :]
            xi = turned[at + 8 : at + 16, :]
            real.append(xr * c - xi * sn)
            imag.append(xr * sn + xi * c)
        both = jnp.concatenate(real + imag, axis=0)
        hi, lo = split(both)
        top = basis_ref[0, par]
        prod = (
            jnp.dot(hi, top, preferred_element_type=F32)
            + jnp.dot(lo, top, preferred_element_type=F32)
            + jnp.dot(hi, basis_ref[1, par], preferred_element_type=F32)
        )
        halves.append((prod[:32, :256] - prod[32:, 256:], prod[:32, 256:] + prod[32:, :256]))
    (er, ei), (orr, oi) = halves
    for b in range(4):
        rows = slice(b * 8, b * 8 + 6)
        o_ref[b, :, 0:256] = er[rows] + orr[rows]
        o_ref[b, :, 256:512] = er[rows] - orr[rows]
        o_ref[b, :, 512:768] = ei[rows] + oi[rows]
        o_ref[b, :, 768:1024] = ei[rows] - oi[rows]


def body(samples, filter_taps, feed_cylinder, feed_delay, pointing, chirp_rate):
    tail = lax.ppermute(samples[:, 3 * 2 * NCHAN :], "tm", [(0, 1)])
    big = pltpu.CompilerParams(vmem_limit_bytes=56 * 2**20)
    sent = pl.pallas_call(
        dft_kernel,
        out_shape=jax.ShapeDtypeStruct((2, NDEV, 2, 128), BF),
        in_specs=[VMEM] * 4, out_specs=VMEM,
        scratch_shapes=[pltpu.VMEM((2, 128, NCHAN), F32)],
        compiler_params=big,
    )(samples, tail, filter_taps, jnp.asarray(forward_rows()))
    got = exchange(sent, 0)
    formed = pl.pallas_call(
        beam_kernel,
        out_shape=jax.ShapeDtypeStruct((64, BEAMS), F32),
        in_specs=[VMEM] * 4, out_specs=VMEM,
        scratch_shapes=[
            pltpu.VMEM((2, FEEDS, 2 * BEAMS), BF),
            pltpu.VMEM((2 * NDEV, 128), F32),
            pltpu.VMEM((512, 128), F32),
            pltpu.VMEM((32, FEEDS), BF),
        ],
        compiler_params=big,
    )(got, feed_delay.reshape(GROUPS, 16), feed_cylinder.reshape(GROUPS, 16), pointing.T)
    packed = pl.pallas_call(
        pack_kernel,
        out_shape=jax.ShapeDtypeStruct((NDEV, 2, 128), BF),
        in_specs=[VMEM], out_specs=VMEM,
        scratch_shapes=[pltpu.VMEM((512, 128), F32), pltpu.VMEM((512, 128), F32)],
        compiler_params=big,
    )(formed)
    back = exchange(packed, 1)
    return pl.pallas_call(
        synth_kernel,
        out_shape=jax.ShapeDtypeStruct((4, 6, 2 * NCHAN), F32),
        in_specs=[VMEM, pl.BlockSpec(memory_space=pltpu.SMEM), VMEM], out_specs=VMEM,
        scratch_shapes=[pltpu.VMEM((2 * NDEV, 128), F32), pltpu.VMEM((128, 256), F32)],
        compiler_params=big,
    )(back, chirp_rate, jnp.asarray(inverse_rows()))


def solution(mesh):
    return jax.shard_map(
        body,
        mesh=mesh,
        in_specs=(P("feed", "tm"), P(), P(), P(), P(), P("feed")),
        out_specs=P("feed", "tm", None),
        check_vma=False,
    )
```

```python
import math

import jax
import jax.numpy as jnp
import numpy as np
from jax import lax
from jax.experimental import pallas as pl
from jax.experimental.pallas import tpu as pltpu
from jax.sharding import PartitionSpec as P

FEEDS = 2048
NCHAN = 512
BEAMS = 512
TAPS = 4
CYL = 4
PHASES = 4096
GROUPS = 128
NDEV = 256
MESH = pl.DeviceIdType.MESH
BF = jnp.bfloat16
F32 = jnp.float32
VMEM = pl.BlockSpec(memory_space=pltpu.VMEM)

def _fit():
    grid = np.cos(np.pi * (np.arange(4000) + 0.5) / 8000) * 0.5
    sq = grid * grid
    sine = np.sin(np.pi * grid) / grid * math.sqrt(2.0)
    cosine = np.cos(np.pi * grid) * math.sqrt(2.0)
    mat = np.stack([sq**k for k in range(5)], axis=1)
    s = np.linalg.lstsq(mat * grid[:, None], sine * grid, rcond=None)[0]
    c = np.linalg.lstsq(mat, cosine, rcond=None)[0]
    return [float(v) for v in s], [float(v) for v in c]


SIN_C, COS_C = _fit()
ROUND = 1.5 * 2.0**23
EARLY = 17
PER = 17


def cos_sin(turns):
    r = turns - ((turns + ROUND) - ROUND)
    q = r * r
    s = SIN_C[4]
    c = COS_C[4]
    for k in (3, 2, 1, 0):
        s = s * q + SIN_C[k]
        c = c * q + COS_C[k]
    s = s * r
    return 1.0 - s * s, s * c


def split_const(x):
    hi = x.astype(np.float32).astype(BF)
    lo = (x - hi.astype(np.float64)).astype(np.float32).astype(BF)
    return np.stack([hi, lo])


def forward_rows():
    n = np.arange(NCHAN)[None, :]
    out = []
    for par in range(2):
        c = 2 * np.arange(NCHAN // 2)[:, None] + par
        ang = (n * c % (2 * NCHAN)) * (2.0 * np.pi / (2 * NCHAN))
        both = np.stack([np.cos(ang), -np.sin(ang)], axis=1) / math.sqrt(2 * NCHAN)
        out.append(both.reshape(NCHAN, NCHAN))
    return split_const(np.stack(out))


def inverse_rows():
    t = np.arange(NCHAN // 2)[None, :]
    out = []
    for par in range(2):
        c = 2 * np.arange(NCHAN // 2)[:, None] + par
        ang = (t * c % NCHAN) * (2.0 * np.pi / NCHAN)
        out.append(np.concatenate([np.cos(ang), np.sin(ang)], axis=1) / math.sqrt(NCHAN))
    return split_const(np.stack(out))


def split(x):
    hi = x.astype(BF)
    return hi, (x - hi.astype(F32)).astype(BF)


def nt(a, b):
    return lax.dot_general(a, b, (((1,), (1,)), ((), ())), preferred_element_type=F32)


def main_kernel(
    x_ref, taps_ref, delay_ref, cyl_ref, point_ref, basis_ref, back_ref,
    tail, basis, fold, sent, got, weights, cols, table, wide, turned, lhs, flip, pairs, packed,
    load_sem, halo_send, halo_recv, ready, send_sem, recv_sem,
):
    length = 2 * NCHAN
    feed = lax.axis_index("feed")
    tm = lax.axis_index("tm")
    me = tm * GROUPS + feed
    plane = lax.rem(feed // 2, 16)
    ring = tm * 8 + feed // 32 * 2 + lax.rem(feed, 2)

    def at(ring, plane):
        return lax.rem(ring // 2, 4) * 32 + plane * 2 + lax.rem(ring, 2), ring // 8

    load = pltpu.make_async_copy(basis_ref, basis, load_sem)
    load.start()
    barrier = pltpu.get_barrier_semaphore()
    for k in range(1, 16):
        for where in (at(ring ^ k, plane), at(ring, plane ^ k)):
            pl.semaphore_signal(barrier, inc=1, device_id=where, device_id_type=MESH)

    delay = delay_ref[...].astype(F32)
    cyl = cyl_ref[...].astype(F32)
    for par in range(2):
        t = (2 * me + par + 1).astype(F32) * delay
        t = t - jnp.floor(t * (1.0 / PHASES)) * PHASES
        for g in range(8):
            cols[par, pl.ds(g, 16, stride=8), :] = pltpu.roll(t, (128 - 16 * g) % 128, 1)
    for g in range(8):
        cols[2, pl.ds(g, 16, stride=8), :] = pltpu.roll(cyl, (128 - 16 * g) % 128, 1)
    for q in range(4):
        table[q, 0:4, :] = point_ref[:, q * 128 : q * 128 + 128].astype(F32) * (1.0 / PHASES)
    fold[...] = jnp.zeros_like(fold)

    pl.semaphore_wait(barrier, 30)
    for k in range(1, 16):
        pl.semaphore_signal(ready, inc=1, device_id=at(ring, plane ^ k), device_id_type=MESH)
    halo = pltpu.make_async_remote_copy(
        src_ref=x_ref.at[:, pl.ds(3 * length, 3 * length)], dst_ref=tail,
        send_sem=halo_send, recv_sem=halo_recv, device_id=(feed, 1), device_id_type=MESH,
    )

    @pl.when(tm == 0)
    def _():
        halo.start()
        tail[...] = jnp.zeros_like(tail)

    def make(step):
        i, half = step // 2, lax.rem(step, 2)
        shift = lax.rem(128 - i, 128)
        for rc in range(4):
            rows = slice(rc * 32, rc * 32 + 32)
            t0, t1, kind = [
                jnp.broadcast_to(pltpu.roll(cols[n, rows, :], shift, 1)[:, 0:1], (32, 128)) for n in range(3)
            ]
            for j in range(2):
                q = half * 2 + j
                p = [table[q, k : k + 1, :] for k in range(4)]
                steer = jnp.where(kind == 0.0, p[0], jnp.where(kind == 1.0, p[1], jnp.where(kind == 2.0, p[2], p[3])))
                for par, t in ((0, t0), (1, t1)):
                    c, s = cos_sin(t * steer)
                    at_rows = pl.ds(pl.multiple_of(i * 128 + rc * 32, 32), 32)
                    weights[par, q, at_rows, 0:128] = c.astype(BF)
                    weights[par, q, at_rows, 128:256] = s.astype(BF)

    def early(step, carry):
        make(step)
        return carry

    lax.fori_loop(0, EARLY, early, 0)
    load.wait()

    @pl.when(tm == 1)
    def _():
        halo.wait_recv()

    for f in range(6):
        acc = None
        for k in range(TAPS):
            src = f + k - 3
            if src < 0:
                piece = tail[:, (src + 3) * length : (src + 4) * length]
            else:
                piece = x_ref[:, src * length : (src + 1) * length]
            term = taps_ref[k : k + 1, :] * piece.astype(F32)
            acc = term if acc is None else acc + term
        a, b = acc[:, :NCHAN], acc[:, NCHAN:]
        fold[0, f * 16 : f * 16 + 16, :] = a + b
        fold[1, f * 16 : f * 16 + 16, :] = a - b
    for par in range(2):
        hi, lo = split(fold[par])
        top = basis[0, par]
        out = nt(top, hi) + nt(top, lo) + nt(basis[1, par], hi)
        sent[par] = out.astype(BF).reshape(NDEV, 2, 128)

    @pl.when(tm == 0)
    def _():
        halo.wait_send()

    pl.semaphore_wait(ready, 15)

    def late(step, carry):
        for n in range(PER):
            k = 1 + step * PER + n
            f, t = lax.rem(feed + k, GROUPS), lax.rem(tm + (feed + k) // GROUPS, 2)
            pltpu.make_async_remote_copy(
                src_ref=sent.at[:, t * GROUPS + f], dst_ref=got.at[:, me],
                send_sem=send_sem.at[0], recv_sem=recv_sem.at[0], device_id=(f, t), device_id_type=MESH,
            ).start()
        make(EARLY + step)
        return carry

    lax.fori_loop(0, 32 - EARLY, late, 0)
    got[:, me] = sent[:, me]
    pltpu.make_async_remote_copy(
        src_ref=sent.at[:, pl.ds(0, NDEV - 1)], dst_ref=got.at[:, pl.ds(0, NDEV - 1)],
        send_sem=send_sem.at[0], recv_sem=recv_sem.at[0], device_id=(feed, tm), device_id_type=MESH,
    ).wait()

    for par in range(2):
        wide[...] = got[par].astype(F32).reshape(2 * NDEV, 128)
        for ri in range(2):
            for t in range(2):
                block = wide[pl.ds(t * 256 + ri, 128, stride=2), :]
                turned[(ri * 2 + t) * 128 : (ri * 2 + t) * 128 + 128, :] = block.T
        for i in range(16):
            lhs[par, :, i * 128 : i * 128 + 128] = turned[pl.ds(i, 32, stride=16), :].astype(BF)

    pairs[...] = jnp.zeros_like(pairs)
    scale = 1.0 / math.sqrt(FEEDS)
    lane = lax.broadcasted_iota(jnp.int32, (32, 128), 1) // 32

    def chunk(step, carry):
        q = lax.rem(step + feed // 32, 4)
        parts = []
        for par in range(2):
            prod = jnp.dot(lhs[par], weights[par, q], preferred_element_type=F32)
            real = (prod[:16, :128] - prod[16:, 128:]) * scale
            imag = (prod[:16, 128:] + prod[16:, :128]) * scale
            parts.append((real, imag))
        rows = [parts[par][ri][t * 8 : t * 8 + 8] for t in range(2) for par in range(2) for ri in range(2)]
        flip[...] = jnp.concatenate(rows + [jnp.zeros((64, 128), F32)], axis=0).T
        for t in range(2):
            acc = None
            for b in range(4):
                moved = flip[pl.ds(b, 32, stride=4), :]
                if b != t:
                    moved = pltpu.roll(moved, (32 * (b - t)) % 128, 1)
                acc = moved if acc is None else jnp.where(lane == b, moved, acc)
            pairs[pl.ds(0, 32, stride=2), :] = acc
            packed[pl.ds(t * GROUPS + q * 32, 32)] = pairs[...].astype(BF).reshape(32, 2, 128)

        def send(n, carry):
            v = lax.rem(n + feed, 64)
            t, f = v // 32, q * 32 + lax.rem(v, 32)
            to = t * GROUPS + f

            @pl.when(to != me)
            def _():
                pltpu.make_async_remote_copy(
                    src_ref=packed.at[to], dst_ref=back_ref.at[me],
                    send_sem=send_sem.at[1], recv_sem=recv_sem.at[1], device_id=(f, t), device_id_type=MESH,
                ).start()

            return carry

        lax.fori_loop(0, 64, send, 0, unroll=16)
        return carry

    lax.fori_loop(0, 4, chunk, 0)
    back_ref[me] = packed[me]
    pltpu.make_async_remote_copy(
        src_ref=packed.at[pl.ds(0, NDEV - 1)], dst_ref=back_ref.at[pl.ds(0, NDEV - 1)],
        send_sem=send_sem.at[1], recv_sem=recv_sem.at[1], device_id=(feed, tm), device_id_type=MESH,
    ).wait()


def synth_kernel(q_ref, rate_ref, basis_ref, o_ref, wide, turned):
    wide[...] = q_ref[...].astype(F32).reshape(2 * NDEV, 128)
    for h in range(2):
        turned[:, h * 128 : h * 128 + 128] = wide[pl.ds(h * 256, 128, stride=2), :].T
    s = lax.broadcasted_iota(jnp.int32, (8, 256), 1)
    halves = []
    for par in range(2):
        pos = (2 * s + par).astype(F32) * (1.0 / NCHAN)
        real, imag = [], []
        for b in range(4):
            c, sn = cos_sin((0.5 * rate_ref[b]) * (pos * pos))
            at = b * 32 + par * 16
            xr = turned[at : at + 8, :]
            xi = turned[at + 8 : at + 16, :]
            real.append(xr * c - xi * sn)
            imag.append(xr * sn + xi * c)
        both = jnp.concatenate(real + imag, axis=0)
        hi, lo = split(both)
        top = basis_ref[0, par]
        prod = (
            jnp.dot(hi, top, preferred_element_type=F32)
            + jnp.dot(lo, top, preferred_element_type=F32)
            + jnp.dot(hi, basis_ref[1, par], preferred_element_type=F32)
        )
        halves.append((prod[:32, :256] - prod[32:, 256:], prod[:32, 256:] + prod[32:, :256]))
    (er, ei), (orr, oi) = halves
    for b in range(4):
        rows = slice(b * 8, b * 8 + 6)
        o_ref[:, b, 0:256] = er[rows] + orr[rows]
        o_ref[:, b, 256:512] = er[rows] - orr[rows]
        o_ref[:, b, 512:768] = ei[rows] + oi[rows]
        o_ref[:, b, 768:1024] = ei[rows] - oi[rows]


def body(samples, filter_taps, feed_cylinder, feed_delay, pointing, chirp_rate):
    back = pl.pallas_call(
        main_kernel,
        out_shape=jax.ShapeDtypeStruct((NDEV, 2, 128), BF),
        in_specs=[VMEM] * 5 + [pl.BlockSpec(memory_space=pl.ANY)], out_specs=VMEM,
        scratch_shapes=[
            pltpu.VMEM((16, 3 * 2 * NCHAN), BF),
            pltpu.VMEM((2, 2, NCHAN, NCHAN), BF),
            pltpu.VMEM((2, 128, NCHAN), F32),
            pltpu.VMEM((2, NDEV, 2, 128), BF),
            pltpu.VMEM((2, NDEV, 2, 128), BF),
            pltpu.VMEM((2, 4, FEEDS, 256), BF),
            pltpu.VMEM((3, GROUPS, 128), F32),
            pltpu.VMEM((4, 8, 128), F32),
            pltpu.VMEM((2 * NDEV, 128), F32),
            pltpu.VMEM((512, 128), F32),
            pltpu.VMEM((2, 32, FEEDS), BF),
            pltpu.VMEM((128, 128), F32),
            pltpu.VMEM((64, 128), F32),
            pltpu.VMEM((NDEV, 2, 128), BF),
            pltpu.SemaphoreType.DMA,
            pltpu.SemaphoreType.DMA,
            pltpu.SemaphoreType.DMA,
            pltpu.SemaphoreType.REGULAR,
            pltpu.SemaphoreType.DMA((2,)),
            pltpu.SemaphoreType.DMA((2,)),
        ],
        compiler_params=pltpu.CompilerParams(collective_id=0, has_side_effects=True, vmem_limit_bytes=40 * 2**20),
    )(samples, filter_taps, feed_delay.reshape(16, 128), feed_cylinder.reshape(16, 128), pointing.T, jnp.asarray(forward_rows()))
    series = pl.pallas_call(
        synth_kernel,
        out_shape=jax.ShapeDtypeStruct((6, 4, 2 * NCHAN), F32),
        in_specs=[VMEM, pl.BlockSpec(memory_space=pltpu.SMEM), VMEM], out_specs=VMEM,
        scratch_shapes=[pltpu.VMEM((2 * NDEV, 128), F32), pltpu.VMEM((128, 256), F32)],
        compiler_params=pltpu.CompilerParams(vmem_limit_bytes=16 * 2**20),
    )(back, chirp_rate, jnp.asarray(inverse_rows()))
    return jnp.transpose(series, (1, 0, 2))


def solution(mesh):
    return jax.shard_map(
        body,
        mesh=mesh,
        in_specs=(P("feed", "tm"), P(), P(), P(), P(), P("feed")),
        out_specs=P("feed", "tm", None),
        check_vma=False,
    )
```

```python
import math

import jax
import jax.numpy as jnp
import numpy as np
from jax import lax
from jax.experimental import pallas as pl
from jax.experimental.pallas import tpu as pltpu
from jax.sharding import PartitionSpec as P

FEEDS = 2048
NCHAN = 512
BEAMS = 512
TAPS = 4
CYL = 4
PHASES = 4096
GROUPS = 128
NDEV = 256
MESH = pl.DeviceIdType.MESH
BF = jnp.bfloat16
F32 = jnp.float32
VMEM = pl.BlockSpec(memory_space=pltpu.VMEM)

def _fit():
    grid = np.cos(np.pi * (np.arange(4000) + 0.5) / 8000) * 0.5
    sq = grid * grid
    sine = np.sin(np.pi * grid) / grid * math.sqrt(2.0)
    cosine = np.cos(np.pi * grid) * math.sqrt(2.0)
    mat = np.stack([sq**k for k in range(5)], axis=1)
    s = np.linalg.lstsq(mat * grid[:, None], sine * grid, rcond=None)[0]
    c = np.linalg.lstsq(mat, cosine, rcond=None)[0]
    return [float(v) for v in s], [float(v) for v in c]


SIN_C, COS_C = _fit()
ROUND = 1.5 * 2.0**23
MAIN_VMEM = 62 * 2**20
PER = 17
MULT = 37


def cos_sin(turns):
    r = turns - ((turns + ROUND) - ROUND)
    q = r * r
    s = SIN_C[4]
    c = COS_C[4]
    for k in (3, 2, 1, 0):
        s = s * q + SIN_C[k]
        c = c * q + COS_C[k]
    s = s * r
    return 1.0 - s * s, s * c


def split_const(x):
    hi = x.astype(np.float32).astype(BF)
    lo = (x - hi.astype(np.float64)).astype(np.float32).astype(BF)
    return np.stack([hi, lo])


def forward_rows():
    n = np.arange(NCHAN)[None, :]
    out = []
    for par in range(2):
        c = 2 * np.arange(NCHAN // 2)[:, None] + par
        ang = (n * c % (2 * NCHAN)) * (2.0 * np.pi / (2 * NCHAN))
        both = np.stack([np.cos(ang), -np.sin(ang)], axis=1) / math.sqrt(2 * NCHAN)
        out.append(both.reshape(NCHAN, NCHAN))
    return split_const(np.stack(out))


def inverse_rows():
    t = np.arange(NCHAN // 2)[None, :]
    out = []
    for par in range(2):
        c = 2 * np.arange(NCHAN // 2)[:, None] + par
        ang = (t * c % NCHAN) * (2.0 * np.pi / NCHAN)
        out.append(np.concatenate([np.cos(ang), np.sin(ang)], axis=1) / math.sqrt(NCHAN))
    return split_const(np.stack(out))


def split(x):
    hi = x.astype(BF)
    return hi, (x - hi.astype(F32)).astype(BF)


def nt(a, b):
    return lax.dot_general(a, b, (((1,), (1,)), ((), ())), preferred_element_type=F32)


def main_kernel(
    x_hbm, taps_hbm, delay_hbm, cyl_hbm, point_hbm, basis_hbm, back_ref,
    x_ref, taps_ref, delay_ref, cyl_ref, point_ref, basis, fold, sent, got, weights, cols, table, wide, turned, lhs, flip, pairs, packed,
    load_sem, ready, send_sem, recv_sem,
):
    length = 2 * NCHAN
    feed = lax.axis_index("feed")
    tm = lax.axis_index("tm")
    me = tm * GROUPS + feed
    plane = lax.rem(feed // 2, 16)
    ring = tm * 8 + feed // 32 * 2 + lax.rem(feed, 2)

    def at(ring, plane):
        return lax.rem(ring // 2, 4) * 32 + plane * 2 + lax.rem(ring, 2), ring // 8

    loads = [
        pltpu.make_async_copy(src, dst, load_sem.at[n])
        for n, (src, dst) in enumerate(
            ((delay_hbm, delay_ref), (cyl_hbm, cyl_ref), (point_hbm, point_ref), (x_hbm, x_ref), (taps_hbm, taps_ref), (basis_hbm, basis))
        )
    ]
    for load in loads:
        load.start()
    barrier = pltpu.get_barrier_semaphore()
    for k in range(1, 16):
        for where in (at(ring ^ k, plane), at(ring, plane ^ k)):
            pl.semaphore_signal(barrier, inc=1, device_id=where, device_id_type=MESH)

    for load in loads[:3]:
        load.wait()
    delay = delay_ref[...].astype(F32)
    cyl = cyl_ref[...].astype(F32)
    for par in range(2):
        t = (2 * me + par + 1).astype(F32) * delay
        t = t - jnp.floor(t * (1.0 / PHASES)) * PHASES
        for g in range(8):
            cols[par, pl.ds(g, 16, stride=8), :] = pltpu.roll(t, (128 - 16 * g) % 128, 1)
    for g in range(8):
        cols[2, pl.ds(g, 16, stride=8), :] = pltpu.roll(cyl, (128 - 16 * g) % 128, 1)
    for q in range(4):
        table[q, 0:4, :] = point_ref[:, q * 128 : q * 128 + 128].astype(F32) * (1.0 / PHASES)

    loads[3].wait()
    pl.semaphore_wait(barrier, 30)
    for k in range(1, 16):
        pl.semaphore_signal(ready, inc=1, device_id=at(ring, plane ^ k), device_id_type=MESH)

    def make(step):
        i, half = step // 2, lax.rem(step, 2)
        shift = lax.rem(128 - i, 128)
        for rc in range(4):
            rows = slice(rc * 32, rc * 32 + 32)
            t0, t1, kind = [
                jnp.broadcast_to(pltpu.roll(cols[n, rows, :], shift, 1)[:, 0:1], (32, 128)) for n in range(3)
            ]
            for j in range(2):
                q = half * 2 + j
                p = [table[q, k : k + 1, :] for k in range(4)]
                steer = jnp.where(kind == 0.0, p[0], jnp.where(kind == 1.0, p[1], jnp.where(kind == 2.0, p[2], p[3])))
                for par, t in ((0, t0), (1, t1)):
                    c, s = cos_sin(t * steer)
                    at_rows = pl.ds(pl.multiple_of(i * 128 + rc * 32, 32), 32)
                    weights[par, q, at_rows, 0:128] = c.astype(BF)
                    weights[par, q, at_rows, 128:256] = s.astype(BF)

    for load in loads[4:]:
        load.wait()
    for f in range(9):
        acc = None
        for k in range(TAPS):
            src = f + k - 3
            if 0 <= src < 6:
                term = taps_ref[k : k + 1, :] * x_ref[:, src * length : (src + 1) * length].astype(F32)
                acc = term if acc is None else acc + term
        a, b = acc[:, :NCHAN], acc[:, NCHAN:]
        fold[0, f * 16 : f * 16 + 16, :] = a + b
        fold[1, f * 16 : f * 16 + 16, :] = a - b
    extra = None
    for par in range(2):
        hi, lo = split(fold[par])
        top = basis[0, par]
        out = nt(top, hi) + nt(top, lo) + nt(basis[1, par], hi)
        sent[:, par, :, :] = out[:, :128].astype(BF).reshape(NDEV, 2, 128)
        wide[0 : 2 * NDEV, 0:16] = out[:, 128:144]
        for ri in range(2):
            spot = 16 * (2 * par + ri)
            moved = wide[pl.ds(ri, NDEV, stride=2), :]
            if spot:
                moved = pltpu.roll(moved, spot, 1)
            where = lax.broadcasted_iota(jnp.int32, (NDEV, 128), 1) // 16 == 2 * par + ri
            extra = jnp.where(where, moved, 0.0 if extra is None else extra)
    wide[pl.ds(0, NDEV, stride=2), :] = extra
    sent[:, 2, :, :] = wide[0 : 2 * NDEV, :].astype(BF).reshape(NDEV, 2, 128)

    def rest(step, carry):
        make(step)
        return carry

    pl.semaphore_wait(ready, 15)

    def start(half, k):
        to = (me + k * MULT) & (NDEV - 1)
        f, t = to & (GROUPS - 1), to >> 7

        pltpu.make_async_remote_copy(
            src_ref=sent.at[to, pl.ds(0, 3 - half)], dst_ref=got.at[me, pl.ds(0, 3 - half)],
            send_sem=send_sem.at[0], recv_sem=recv_sem.at[half], device_id=(f, t), device_id_type=MESH,
        ).start()

    for half in range(2):

        @pl.when(tm == half)
        def _():
            def group(step, carry):
                for n in range(PER):
                    start(half, 1 + step * PER + n)
                return carry

            lax.fori_loop(0, 255 // PER, group, 0)

    own = [
        pltpu.make_async_copy(sent.at[me], got.at[me], recv_sem.at[0]),
        pltpu.make_async_copy(sent.at[me, pl.ds(0, 2)], got.at[me, pl.ds(0, 2)], recv_sem.at[1]),
    ]
    for t in range(2):
        pl.when(tm == t)(own[t].start)
    lax.fori_loop(0, 32, rest, 0)

    def whole(count, t):
        size = 3 - t
        return pltpu.make_async_remote_copy(
            src_ref=sent.at[pl.ds(0, count), pl.ds(0, size)], dst_ref=got.at[pl.ds(0, count), pl.ds(0, size)],
            send_sem=send_sem.at[0], recv_sem=recv_sem.at[t], device_id=(feed, tm), device_id_type=MESH,
        )

    for t in range(2):
        whole(GROUPS, t).wait_recv()
        pl.when(tm == t)(whole(NDEV - 1, t).wait_send)
    for par in range(2):
        wide[...] = got[:, par].astype(F32).reshape(2 * NDEV, 128)
        for ri in range(2):
            for t in range(2):
                block = wide[pl.ds(t * 256 + ri, 128, stride=2), :]
                turned[par, (ri * 2 + t) * 128 : (ri * 2 + t) * 128 + 128, :] = block.T
    wide[0:256, :] = got[0:GROUPS, 2].astype(F32).reshape(256, 128)
    block = wide[pl.ds(0, 128, stride=2), :].T
    for par in range(2):
        for ri in range(2):
            turned[par, (ri * 2 + 1) * 128 + 96 : (ri * 2 + 1) * 128 + 112, :] = block[(par * 2 + ri) * 16 : (par * 2 + ri) * 16 + 16]
        for i in range(16):
            lhs[par, :, i * 128 : i * 128 + 128] = turned[par, pl.ds(i, 32, stride=16), :].astype(BF)

    pairs[...] = jnp.zeros_like(pairs)
    scale = 1.0 / math.sqrt(FEEDS)
    lane = lax.broadcasted_iota(jnp.int32, (32, 128), 1) // 32

    unit = lax.broadcasted_iota(jnp.int32, (8, 128), 0)

    def whole_frames(x):
        first, second = x[:8], x[8:]
        terms = jnp.where(unit == 2, pltpu.roll(second, 4, 0), pltpu.roll(first, 2, 0))
        return first * scale, (second + jnp.where(unit < 3, terms, 0.0)) * scale

    def chunk(step, carry):
        q = (feed // 32 + jnp.where(step == 2, 3, jnp.where(step == 3, 2, step))) & 3
        parts = []
        for par in range(2):
            prod = jnp.dot(lhs[par], weights[par, q], preferred_element_type=F32)
            real = prod[:16, :128] - prod[16:, 128:]
            imag = prod[:16, 128:] + prod[16:, :128]
            parts.append((whole_frames(real), whole_frames(imag)))
        rows = [parts[par][ri][t] for t in range(2) for par in range(2) for ri in range(2)]
        flip[...] = jnp.concatenate(rows + [jnp.zeros((64, 128), F32)], axis=0).T
        for t in range(2):
            acc = None
            for b in range(4):
                moved = flip[pl.ds(b, 32, stride=4), :]
                if b != t:
                    moved = pltpu.roll(moved, (32 * (b - t)) % 128, 1)
                acc = moved if acc is None else jnp.where(lane == b, moved, acc)
            pairs[pl.ds(0, 32, stride=2), :] = acc
            packed[pl.ds(t * GROUPS + q * 32, 32)] = pairs[...].astype(BF).reshape(32, 2, 128)

        def send(n, carry):
            v = (n + feed) & 63
            t, f = v >> 5, q * 32 + (v & 31)
            to = t * GROUPS + f

            @pl.when(to != me)
            def _():
                pltpu.make_async_remote_copy(
                    src_ref=packed.at[to], dst_ref=back_ref.at[me],
                    send_sem=send_sem.at[1], recv_sem=recv_sem.at[2], device_id=(f, t), device_id_type=MESH,
                ).start()

            return carry

        lax.fori_loop(0, 64, send, 0, unroll=16)
        return carry

    lax.fori_loop(0, 4, chunk, 0)
    back_ref[me] = packed[me]
    pltpu.make_async_remote_copy(
        src_ref=packed.at[pl.ds(0, NDEV - 1)], dst_ref=back_ref.at[pl.ds(0, NDEV - 1)],
        send_sem=send_sem.at[1], recv_sem=recv_sem.at[2], device_id=(feed, tm), device_id_type=MESH,
    ).wait()


def synth_kernel(q_ref, rate_ref, basis_ref, o_ref, wide, turned):
    wide[...] = q_ref[...].astype(F32).reshape(2 * NDEV, 128)
    for h in range(2):
        turned[:, h * 128 : h * 128 + 128] = wide[pl.ds(h * 256, 128, stride=2), :].T
    s = lax.broadcasted_iota(jnp.int32, (8, 256), 1)
    halves = []
    for par in range(2):
        pos = (2 * s + par).astype(F32) * (1.0 / NCHAN)
        real, imag = [], []
        for b in range(4):
            c, sn = cos_sin((0.5 * rate_ref[b]) * (pos * pos))
            at = b * 32 + par * 16
            xr = turned[at : at + 8, :]
            xi = turned[at + 8 : at + 16, :]
            real.append(xr * c - xi * sn)
            imag.append(xr * sn + xi * c)
        both = jnp.concatenate(real + imag, axis=0)
        hi, lo = split(both)
        top = basis_ref[0, par]
        prod = (
            jnp.dot(hi, top, preferred_element_type=F32)
            + jnp.dot(lo, top, preferred_element_type=F32)
            + jnp.dot(hi, basis_ref[1, par], preferred_element_type=F32)
        )
        halves.append((prod[:32, :256] - prod[32:, 256:], prod[:32, 256:] + prod[32:, :256]))
    (er, ei), (orr, oi) = halves
    for b in range(4):
        rows = slice(b * 8, b * 8 + 6)
        o_ref[:, b, 0:256] = er[rows] + orr[rows]
        o_ref[:, b, 256:512] = er[rows] - orr[rows]
        o_ref[:, b, 512:768] = ei[rows] + oi[rows]
        o_ref[:, b, 768:1024] = ei[rows] - oi[rows]


def body(samples, filter_taps, feed_cylinder, feed_delay, pointing, chirp_rate):
    back = pl.pallas_call(
        main_kernel,
        out_shape=jax.ShapeDtypeStruct((NDEV, 2, 128), BF),
        in_specs=[pl.BlockSpec(memory_space=pl.ANY)] * 6, out_specs=VMEM,
        scratch_shapes=[
            pltpu.VMEM((16, 6 * 2 * NCHAN), BF),
            pltpu.VMEM((TAPS, 2 * NCHAN), F32),
            pltpu.VMEM((16, 128), jnp.int32),
            pltpu.VMEM((16, 128), jnp.int32),
            pltpu.VMEM((CYL, BEAMS), jnp.int32),
            pltpu.VMEM((2, 2, NCHAN, NCHAN), BF),
            pltpu.VMEM((2, 144, NCHAN), F32),
            pltpu.VMEM((NDEV, 3, 2, 128), BF),
            pltpu.VMEM((NDEV, 3, 2, 128), BF),
            pltpu.VMEM((2, 4, FEEDS, 256), BF),
            pltpu.VMEM((3, GROUPS, 128), F32),
            pltpu.VMEM((4, 8, 128), F32),
            pltpu.VMEM((2 * NDEV, 128), F32),
            pltpu.VMEM((2, 512, 128), F32),
            pltpu.VMEM((2, 32, FEEDS), BF),
            pltpu.VMEM((128, 128), F32),
            pltpu.VMEM((64, 128), F32),
            pltpu.VMEM((NDEV, 2, 128), BF),
            pltpu.SemaphoreType.DMA((6,)),
            pltpu.SemaphoreType.REGULAR,
            pltpu.SemaphoreType.DMA((2,)),
            pltpu.SemaphoreType.DMA((3,)),
        ],
        compiler_params=pltpu.CompilerParams(collective_id=0, has_side_effects=True, vmem_limit_bytes=MAIN_VMEM),
    )(samples, filter_taps, feed_delay.reshape(16, 128), feed_cylinder.reshape(16, 128), pointing.T, jnp.asarray(forward_rows()))
    series = pl.pallas_call(
        synth_kernel,
        out_shape=jax.ShapeDtypeStruct((6, 4, 2 * NCHAN), F32),
        in_specs=[VMEM, pl.BlockSpec(memory_space=pltpu.SMEM), VMEM], out_specs=VMEM,
        scratch_shapes=[pltpu.VMEM((2 * NDEV, 128), F32), pltpu.VMEM((128, 256), F32)],
        compiler_params=pltpu.CompilerParams(vmem_limit_bytes=16 * 2**20),
    )(back, chirp_rate, jnp.asarray(inverse_rows()))
    return jnp.transpose(series, (1, 0, 2))


def solution(mesh):
    return jax.shard_map(
        body,
        mesh=mesh,
        in_specs=(P("feed", "tm"), P(), P(), P(), P(), P("feed")),
        out_specs=P("feed", "tm", None),
        check_vma=False,
    )
```

```python
import math

import jax
import jax.numpy as jnp
import numpy as np
from jax import lax
from jax.experimental import pallas as pl
from jax.experimental.pallas import tpu as pltpu
from jax.sharding import PartitionSpec as P

FEEDS = 2048
NCHAN = 512
BEAMS = 512
TAPS = 4
CYL = 4
PHASES = 4096
GROUPS = 128
NDEV = 256
MESH = pl.DeviceIdType.MESH
BF = jnp.bfloat16
F32 = jnp.float32
VMEM = pl.BlockSpec(memory_space=pltpu.VMEM)

def _fit():
    grid = np.cos(np.pi * (np.arange(4000) + 0.5) / 8000) * 0.5
    sq = grid * grid
    sine = np.sin(np.pi * grid) / grid * math.sqrt(2.0)
    cosine = np.cos(np.pi * grid) * math.sqrt(2.0)
    mat = np.stack([sq**k for k in range(5)], axis=1)
    s = np.linalg.lstsq(mat * grid[:, None], sine * grid, rcond=None)[0]
    c = np.linalg.lstsq(mat, cosine, rcond=None)[0]
    return [float(v) for v in s], [float(v) for v in c]


SIN_C, COS_C = _fit()
ROUND = 1.5 * 2.0**23
MAIN_VMEM = 62 * 2**20
EARLY = 6


def cos_sin(turns):
    r = turns - ((turns + ROUND) - ROUND)
    q = r * r
    s = SIN_C[4]
    c = COS_C[4]
    for k in (3, 2, 1, 0):
        s = s * q + SIN_C[k]
        c = c * q + COS_C[k]
    s = s * r
    return 1.0 - s * s, s * c


def split_const(x):
    hi = x.astype(np.float32).astype(BF)
    lo = (x - hi.astype(np.float64)).astype(np.float32).astype(BF)
    return np.stack([hi, lo])


def forward_rows():
    n = np.arange(NCHAN)[None, :]
    out = []
    for par in range(2):
        c = 2 * np.arange(NCHAN // 2)[:, None] + par
        ang = (n * c % (2 * NCHAN)) * (2.0 * np.pi / (2 * NCHAN))
        both = np.stack([np.cos(ang), -np.sin(ang)], axis=1) / math.sqrt(2 * NCHAN)
        out.append(both.reshape(NCHAN, NCHAN))
    return split_const(np.stack(out))


def inverse_rows():
    t = np.arange(NCHAN // 2)[None, :]
    out = []
    for par in range(2):
        c = 2 * np.arange(NCHAN // 2)[:, None] + par
        ang = (t * c % NCHAN) * (2.0 * np.pi / NCHAN)
        out.append(np.concatenate([np.cos(ang), np.sin(ang)], axis=1) / math.sqrt(NCHAN))
    return split_const(np.stack(out))


def split(x):
    hi = x.astype(BF)
    return hi, (x - hi.astype(F32)).astype(BF)


def nt(a, b):
    return lax.dot_general(a, b, (((1,), (1,)), ((), ())), preferred_element_type=F32)


def main_kernel(
    x_hbm, taps_hbm, delay_hbm, cyl_hbm, point_hbm, basis_hbm, inverse_hbm, rate_ref, o_ref,
    x_ref, taps_ref, delay_ref, cyl_ref, point_ref, basis, fold, sent, got, weights, cols, table, wide, turned, lhs, flip, pairs, packed, back_ref, inverse, chirp,
    load_sem, ready, send_sem, recv_sem,
):
    length = 2 * NCHAN
    feed = lax.axis_index("feed")
    tm = lax.axis_index("tm")
    me = tm * GROUPS + feed
    plane = lax.rem(feed // 2, 16)
    ring = tm * 8 + feed // 32 * 2 + lax.rem(feed, 2)

    def at(ring, plane):
        return ((ring >> 1) & 3) * 32 + plane * 2 + (ring & 1), ring >> 3

    loads = [
        pltpu.make_async_copy(src, dst, load_sem.at[n])
        for n, (src, dst) in enumerate(
            ((delay_hbm, delay_ref), (cyl_hbm, cyl_ref), (point_hbm, point_ref), (x_hbm, x_ref), (taps_hbm, taps_ref), (basis_hbm, basis), (inverse_hbm, inverse))
        )
    ]
    for load in loads:
        load.start()
    barrier = pltpu.get_barrier_semaphore()
    for k in range(1, 16):
        for where in (at(ring ^ k, plane), at(ring, plane ^ k)):
            pl.semaphore_signal(barrier, inc=1, device_id=where, device_id_type=MESH)

    for load in loads[:3]:
        load.wait()
    delay = delay_ref[...].astype(F32)
    cyl = cyl_ref[...].astype(F32)
    for par in range(2):
        t = (2 * me + par + 1).astype(F32) * delay
        t = t - jnp.floor(t * (1.0 / PHASES)) * PHASES
        for g in range(8):
            cols[par, pl.ds(g, 16, stride=8), :] = pltpu.roll(t, (128 - 16 * g) % 128, 1)
    for g in range(8):
        cols[2, pl.ds(g, 16, stride=8), :] = pltpu.roll(cyl, (128 - 16 * g) % 128, 1)
    for q in range(4):
        table[q, 0:4, :] = point_ref[:, q * 128 : q * 128 + 128].astype(F32) * (1.0 / PHASES)

    def make(step):
        i, half = step // 2, lax.rem(step, 2)
        shift = lax.rem(128 - i, 128)
        for rc in range(4):
            rows = slice(rc * 32, rc * 32 + 32)
            t0, t1, kind = [
                jnp.broadcast_to(pltpu.roll(cols[n, rows, :], shift, 1)[:, 0:1], (32, 128)) for n in range(3)
            ]
            for j in range(2):
                q = half * 2 + j
                p = [table[q, k : k + 1, :] for k in range(4)]
                steer = jnp.where(kind == 0.0, p[0], jnp.where(kind == 1.0, p[1], jnp.where(kind == 2.0, p[2], p[3])))
                for par, t in ((0, t0), (1, t1)):
                    c, s = cos_sin(t * steer)
                    at_rows = pl.ds(pl.multiple_of(i * 128 + rc * 32, 32), 32)
                    weights[par, q, 0, at_rows, :] = c.astype(BF)
                    weights[par, q, 1, at_rows, :] = s.astype(BF)

    for load in loads[3:6]:
        load.wait()
    for f in range(9):
        acc = None
        for k in range(TAPS):
            src = f + k - 3
            if 0 <= src < 6:
                term = taps_ref[k : k + 1, :] * x_ref[:, src * length : (src + 1) * length].astype(F32)
                acc = term if acc is None else acc + term
        a, b = acc[:, :NCHAN], acc[:, NCHAN:]
        fold[0, f * 16 : f * 16 + 16, :] = a + b
        fold[1, f * 16 : f * 16 + 16, :] = a - b
    extra = None
    for par in range(2):
        hi, lo = split(fold[par])
        top = basis[0, par]
        out = nt(top, hi) + nt(top, lo) + nt(basis[1, par], hi)
        sent[:, par, :, :] = out[:, :128].astype(BF).reshape(NDEV, 2, 128)
        wide[0 : 2 * NDEV, 0:16] = out[:, 128:144]
        for ri in range(2):
            spot = 16 * (2 * par + ri)
            moved = wide[pl.ds(ri, NDEV, stride=2), :]
            if spot:
                moved = pltpu.roll(moved, spot, 1)
            where = lax.broadcasted_iota(jnp.int32, (NDEV, 128), 1) // 16 == 2 * par + ri
            extra = jnp.where(where, moved, 0.0 if extra is None else extra)
    wide[pl.ds(0, NDEV, stride=2), :] = extra
    sent[:, 2, :, :] = wide[0 : 2 * NDEV, :].astype(BF).reshape(NDEV, 2, 128)

    pl.semaphore_wait(barrier, 30)
    for k in range(1, 16):
        pl.semaphore_signal(ready, inc=1, device_id=at(ring, plane ^ k), device_id_type=MESH)

    def rest(step, carry):
        make(step)
        return carry

    def start(half, where):
        f, t = where
        pltpu.make_async_remote_copy(
            src_ref=sent.at[t * GROUPS + f, pl.ds(0, 3 - half)], dst_ref=got.at[me, pl.ds(0, 3 - half)],
            send_sem=send_sem.at[0], recv_sem=recv_sem.at[half], device_id=where, device_id_type=MESH,
        ).start()

    for half in range(2):

        @pl.when(tm == half)
        def _():
            def known(k, carry):
                start(half, at(ring ^ k, plane))
                start(half, at(ring, plane ^ k))
                return carry

            lax.fori_loop(1, 16, known, 0, unroll=5)

    lax.fori_loop(0, EARLY, rest, 0)
    pl.semaphore_wait(ready, 15)
    for half in range(2):

        @pl.when(tm == half)
        def _():
            def far(k, carry):
                for n in range(1, 16):
                    start(half, at(ring ^ k, plane ^ n))
                return carry

            lax.fori_loop(1, 16, far, 0)

    own = [
        pltpu.make_async_copy(sent.at[me], got.at[me], recv_sem.at[0]),
        pltpu.make_async_copy(sent.at[me, pl.ds(0, 2)], got.at[me, pl.ds(0, 2)], recv_sem.at[1]),
    ]
    for t in range(2):
        pl.when(tm == t)(own[t].start)

    lax.fori_loop(EARLY, 32, rest, 0)

    def whole(count, t):
        size = 3 - t
        return pltpu.make_async_remote_copy(
            src_ref=sent.at[pl.ds(0, count), pl.ds(0, size)], dst_ref=got.at[pl.ds(0, count), pl.ds(0, size)],
            send_sem=send_sem.at[0], recv_sem=recv_sem.at[t], device_id=(feed, tm), device_id_type=MESH,
        )

    for t in range(2):
        whole(GROUPS, t).wait_recv()
        pl.when(tm == t)(whole(NDEV - 1, t).wait_send)
    for par in range(2):
        wide[...] = got[:, par].astype(F32).reshape(2 * NDEV, 128)
        for ri in range(2):
            for t in range(2):
                block = wide[pl.ds(t * 256 + ri, 128, stride=2), :]
                turned[par, (ri * 2 + t) * 128 : (ri * 2 + t) * 128 + 128, :] = block.T
    wide[0:256, :] = got[0:GROUPS, 2].astype(F32).reshape(256, 128)
    block = wide[pl.ds(0, 128, stride=2), :].T
    for par in range(2):
        for ri in range(2):
            turned[par, (ri * 2 + 1) * 128 + 96 : (ri * 2 + 1) * 128 + 112, :] = block[(par * 2 + ri) * 16 : (par * 2 + ri) * 16 + 16]
        for i in range(16):
            lhs[par, :, i * 128 : i * 128 + 128] = turned[par, pl.ds(i, 32, stride=16), :].astype(BF)

    pairs[...] = jnp.zeros_like(pairs)
    scale = 1.0 / math.sqrt(FEEDS)
    lane = lax.broadcasted_iota(jnp.int32, (32, 128), 1) // 32

    unit = lax.broadcasted_iota(jnp.int32, (8, 128), 0)

    def whole_frames(x):
        first, second = x[:8], x[8:]
        terms = jnp.where(unit == 2, pltpu.roll(second, 4, 0), pltpu.roll(first, 2, 0))
        return first * scale, (second + jnp.where(unit < 3, terms, 0.0)) * scale

    def part(step):
        return (feed // 32 + jnp.where(step == 2, 3, jnp.where(step == 3, 2, step))) & 3

    def chunk(q):
        parts = []
        for par in range(2):
            both = jnp.concatenate([weights[par, q, 0], weights[par, q, 1]], axis=1)
            prod = jnp.dot(lhs[par], both, preferred_element_type=F32)
            real = prod[:16, :128] - prod[16:, 128:]
            imag = prod[:16, 128:] + prod[16:, :128]
            parts.append((whole_frames(real), whole_frames(imag)))
        rows = [parts[par][ri][t] for t in range(2) for par in range(2) for ri in range(2)]
        flip[...] = jnp.concatenate(rows + [jnp.zeros((64, 128), F32)], axis=0).T
        for t in range(2):
            acc = None
            for b in range(4):
                moved = flip[pl.ds(b, 32, stride=4), :]
                if b != t:
                    moved = pltpu.roll(moved, (32 * (b - t)) % 128, 1)
                acc = moved if acc is None else jnp.where(lane == b, moved, acc)
            pairs[pl.ds(0, 32, stride=2), :] = acc
            packed[pl.ds(t * GROUPS + q * 32, 32)] = pairs[...].astype(BF).reshape(32, 2, 128)

    def send(q, n):
        v = (n + feed) & 63
        t, f = v >> 5, q * 32 + (v & 31)
        to = t * GROUPS + f

        @pl.when(to != me)
        def _():
            pltpu.make_async_remote_copy(
                src_ref=packed.at[to], dst_ref=back_ref.at[me],
                send_sem=send_sem.at[1], recv_sem=recv_sem.at[2], device_id=(f, t), device_id_type=MESH,
            ).start()

    def later(step, carry):
        for n in range(64):
            send(part(step - 1), n)
        chunk(part(step))
        return carry

    def last(n, carry):
        send(part(jnp.int32(3)), n)
        return carry

    chunk(part(jnp.int32(0)))
    lax.fori_loop(1, 4, later, 0)
    lax.fori_loop(0, 64, last, 0, unroll=16)
    back_ref[me] = packed[me]
    pos_ids = lax.broadcasted_iota(jnp.int32, (8, 256), 1)
    for par in range(2):
        pos = (2 * pos_ids + par).astype(F32) * (1.0 / NCHAN)
        for b in range(4):
            chirp[par, b, 0], chirp[par, b, 1] = cos_sin((0.5 * rate_ref[b]) * (pos * pos))
    loads[6].wait()
    pltpu.make_async_remote_copy(
        src_ref=packed.at[pl.ds(0, NDEV - 1)], dst_ref=back_ref.at[pl.ds(0, NDEV - 1)],
        send_sem=send_sem.at[1], recv_sem=recv_sem.at[2], device_id=(feed, tm), device_id_type=MESH,
    ).wait()

    wide[...] = back_ref[...].astype(F32).reshape(2 * NDEV, 128)
    for h in range(2):
        turned[1, h * 128 : h * 128 + 128, :] = wide[pl.ds(h * 256, 128, stride=2), :].T
    halves = []
    for par in range(2):
        real, imag = [], []
        for b in range(4):
            spot = b * 32 + par * 16
            xr, xi = [
                jnp.concatenate([turned[1, h * 128 + spot + o : h * 128 + spot + o + 8, :] for h in range(2)], axis=1)
                for o in (0, 8)
            ]
            c, sn = chirp[par, b, 0], chirp[par, b, 1]
            real.append(xr * c - xi * sn)
            imag.append(xr * sn + xi * c)
        hi, lo = split(jnp.concatenate(real + imag, axis=0))
        top = inverse[0, par]
        prod = (
            jnp.dot(hi, top, preferred_element_type=F32)
            + jnp.dot(lo, top, preferred_element_type=F32)
            + jnp.dot(hi, inverse[1, par], preferred_element_type=F32)
        )
        halves.append((prod[:32, :256] - prod[32:, 256:], prod[:32, 256:] + prod[32:, :256]))
    (er, ei), (sr, si) = halves
    for b in range(4):
        rows = slice(b * 8, b * 8 + 6)
        o_ref[:, b, 0:256] = er[rows] + sr[rows]
        o_ref[:, b, 256:512] = er[rows] - sr[rows]
        o_ref[:, b, 512:768] = ei[rows] + si[rows]
        o_ref[:, b, 768:1024] = ei[rows] - si[rows]


def body(samples, filter_taps, feed_cylinder, feed_delay, pointing, chirp_rate):
    series = pl.pallas_call(
        main_kernel,
        out_shape=jax.ShapeDtypeStruct((6, 4, 2 * NCHAN), F32),
        in_specs=[pl.BlockSpec(memory_space=pl.ANY)] * 7 + [pl.BlockSpec(memory_space=pltpu.SMEM)], out_specs=VMEM,
        scratch_shapes=[
            pltpu.VMEM((16, 6 * 2 * NCHAN), BF),
            pltpu.VMEM((TAPS, 2 * NCHAN), F32),
            pltpu.VMEM((16, 128), jnp.int32),
            pltpu.VMEM((16, 128), jnp.int32),
            pltpu.VMEM((CYL, BEAMS), jnp.int32),
            pltpu.VMEM((2, 2, NCHAN, NCHAN), BF),
            pltpu.VMEM((2, 144, NCHAN), F32),
            pltpu.VMEM((NDEV, 3, 2, 128), BF),
            pltpu.VMEM((NDEV, 3, 2, 128), BF),
            pltpu.VMEM((2, 4, 2, FEEDS, 128), BF),
            pltpu.VMEM((3, GROUPS, 128), F32),
            pltpu.VMEM((4, 8, 128), F32),
            pltpu.VMEM((2 * NDEV, 128), F32),
            pltpu.VMEM((2, 512, 128), F32),
            pltpu.VMEM((2, 32, FEEDS), BF),
            pltpu.VMEM((128, 128), F32),
            pltpu.VMEM((64, 128), F32),
            pltpu.VMEM((NDEV, 2, 128), BF),
            pltpu.VMEM((NDEV, 2, 128), BF),
            pltpu.VMEM((2, 2, NCHAN // 2, NCHAN), BF),
            pltpu.VMEM((2, 4, 2, 8, 256), F32),
            pltpu.SemaphoreType.DMA((7,)),
            pltpu.SemaphoreType.REGULAR,
            pltpu.SemaphoreType.DMA((2,)),
            pltpu.SemaphoreType.DMA((3,)),
        ],
        compiler_params=pltpu.CompilerParams(collective_id=0, has_side_effects=True, vmem_limit_bytes=MAIN_VMEM),
    )(samples, filter_taps, feed_delay.reshape(16, 128), feed_cylinder.reshape(16, 128), pointing.T, jnp.asarray(forward_rows()), jnp.asarray(inverse_rows()), chirp_rate)
    return jnp.transpose(series, (1, 0, 2))


def solution(mesh):
    return jax.shard_map(
        body,
        mesh=mesh,
        in_specs=(P("feed", "tm"), P(), P(), P(), P(), P("feed")),
        out_specs=P("feed", "tm", None),
        check_vma=False,
    )
```

```python
import math

import jax
import jax.numpy as jnp
import numpy as np
from jax import lax
from jax.experimental import pallas as pl
from jax.experimental.pallas import tpu as pltpu
from jax.sharding import PartitionSpec as P

FEEDS = 2048
NCHAN = 512
BEAMS = 512
TAPS = 4
CYL = 4
PHASES = 4096
GROUPS = 128
NDEV = 256
MESH = pl.DeviceIdType.MESH
BF = jnp.bfloat16
F32 = jnp.float32
VMEM = pl.BlockSpec(memory_space=pltpu.VMEM)

def _fit():
    grid = np.cos(np.pi * (np.arange(4000) + 0.5) / 8000) * 0.5
    sq = grid * grid
    sine = np.sin(np.pi * grid) / grid * math.sqrt(2.0)
    cosine = np.cos(np.pi * grid) * math.sqrt(2.0)
    mat = np.stack([sq**k for k in range(5)], axis=1)
    s = np.linalg.lstsq(mat * grid[:, None], sine * grid, rcond=None)[0]
    c = np.linalg.lstsq(mat, cosine, rcond=None)[0]
    return [float(v) for v in s], [float(v) for v in c]


SIN_C, COS_C = _fit()
ROUND = 1.5 * 2.0**23
MAIN_VMEM = 62 * 2**20
EARLY = 6


def cos_sin(turns):
    r = turns - ((turns + ROUND) - ROUND)
    q = r * r
    s = SIN_C[4]
    c = COS_C[4]
    for k in (3, 2, 1, 0):
        s = s * q + SIN_C[k]
        c = c * q + COS_C[k]
    s = s * r
    return 1.0 - s * s, s * c


def split_const(x):
    hi = x.astype(np.float32).astype(BF)
    lo = (x - hi.astype(np.float64)).astype(np.float32).astype(BF)
    return np.stack([hi, lo])


def forward_rows():
    n = np.arange(NCHAN)[None, :]
    out = []
    for par in range(2):
        c = 2 * np.arange(NCHAN // 2)[:, None] + par
        ang = (n * c % (2 * NCHAN)) * (2.0 * np.pi / (2 * NCHAN))
        both = np.stack([np.cos(ang), -np.sin(ang)], axis=1) / math.sqrt(2 * NCHAN)
        out.append(both.reshape(NCHAN, NCHAN))
    return split_const(np.stack(out))


def inverse_rows():
    t = np.arange(NCHAN // 2)[None, :]
    out = []
    for par in range(2):
        c = 2 * np.arange(NCHAN // 2)[:, None] + par
        ang = (t * c % NCHAN) * (2.0 * np.pi / NCHAN)
        out.append(np.concatenate([np.cos(ang), np.sin(ang)], axis=1) / math.sqrt(NCHAN))
    return split_const(np.stack(out))


def split(x):
    hi = x.astype(BF)
    return hi, (x - hi.astype(F32)).astype(BF)


def nt(a, b):
    return lax.dot_general(a, b, (((1,), (1,)), ((), ())), preferred_element_type=F32)


def main_kernel(
    x_hbm, taps_hbm, delay_hbm, cyl_hbm, point_hbm, basis_hbm, inverse_hbm, rate_ref, o_ref,
    x_ref, taps_ref, delay_ref, cyl_ref, point_ref, basis, fold, sent, got, weights, cols, table, wide, turned, lhs, flip, pairs, packed, back_ref, inverse, chirp,
    load_sem, ready, send_sem, recv_sem,
):
    length = 2 * NCHAN
    feed = lax.axis_index("feed")
    tm = lax.axis_index("tm")
    me = tm * GROUPS + feed
    plane = lax.rem(feed // 2, 16)
    ring = tm * 8 + feed // 32 * 2 + lax.rem(feed, 2)

    def at(ring, plane):
        return ((ring >> 1) & 3) * 32 + plane * 2 + (ring & 1), ring >> 3

    loads = [
        pltpu.make_async_copy(src, dst, load_sem.at[n])
        for n, (src, dst) in enumerate(
            ((delay_hbm, delay_ref), (cyl_hbm, cyl_ref), (point_hbm, point_ref), (x_hbm, x_ref), (taps_hbm, taps_ref), (basis_hbm, basis), (inverse_hbm, inverse))
        )
    ]
    for load in loads:
        load.start()
    barrier = pltpu.get_barrier_semaphore()
    for k in range(1, 16):
        for where in (at(ring ^ k, plane), at(ring, plane ^ k)):
            pl.semaphore_signal(barrier, inc=1, device_id=where, device_id_type=MESH)

    for load in loads[:3]:
        load.wait()
    delay = delay_ref[...].astype(F32)
    cyl = cyl_ref[...].astype(F32)
    for par in range(2):
        t = (2 * me + par + 1).astype(F32) * delay
        t = t - jnp.floor(t * (1.0 / PHASES)) * PHASES
        for g in range(8):
            cols[par, pl.ds(g, 16, stride=8), :] = pltpu.roll(t, (128 - 16 * g) % 128, 1)
    for g in range(8):
        cols[2, pl.ds(g, 16, stride=8), :] = pltpu.roll(cyl, (128 - 16 * g) % 128, 1)
    for q in range(4):
        table[q, 0:4, :] = point_ref[:, q * 128 : q * 128 + 128].astype(F32) * (1.0 / PHASES)

    def make(step):
        i, half = step // 2, lax.rem(step, 2)
        shift = lax.rem(128 - i, 128)
        for rc in range(4):
            rows = slice(rc * 32, rc * 32 + 32)
            t0, t1, kind = [
                jnp.broadcast_to(pltpu.roll(cols[n, rows, :], shift, 1)[:, 0:1], (32, 128)) for n in range(3)
            ]
            for j in range(2):
                q = half * 2 + j
                p = [table[q, k : k + 1, :] for k in range(4)]
                steer = jnp.where(kind == 0.0, p[0], jnp.where(kind == 1.0, p[1], jnp.where(kind == 2.0, p[2], p[3])))
                for par, t in ((0, t0), (1, t1)):
                    c, s = cos_sin(t * steer)
                    at_rows = pl.ds(pl.multiple_of(i * 128 + rc * 32, 32), 32)
                    weights[par, q, 0, at_rows, :] = c.astype(BF)
                    weights[par, q, 1, at_rows, :] = s.astype(BF)

    for load in loads[3:6]:
        load.wait()
    for f in range(9):
        acc = None
        for k in range(TAPS):
            src = f + k - 3
            if 0 <= src < 6:
                term = taps_ref[k : k + 1, :] * x_ref[:, src * length : (src + 1) * length].astype(F32)
                acc = term if acc is None else acc + term
        a, b = acc[:, :NCHAN], acc[:, NCHAN:]
        fold[0, f * 16 : f * 16 + 16, :] = a + b
        fold[1, f * 16 : f * 16 + 16, :] = a - b
    extra = None
    for par in range(2):
        hi, lo = split(fold[par])
        top = basis[0, par]
        out = nt(top, hi) + nt(top, lo) + nt(basis[1, par], hi)
        sent[:, par, :, :] = out[:, :128].astype(BF).reshape(NDEV, 2, 128)
        wide[0 : 2 * NDEV, 0:16] = out[:, 128:144]
        for ri in range(2):
            spot = 16 * (2 * par + ri)
            moved = wide[pl.ds(ri, NDEV, stride=2), :]
            if spot:
                moved = pltpu.roll(moved, spot, 1)
            where = lax.broadcasted_iota(jnp.int32, (NDEV, 128), 1) // 16 == 2 * par + ri
            extra = jnp.where(where, moved, 0.0 if extra is None else extra)
    wide[pl.ds(0, NDEV, stride=2), :] = extra
    sent[:, 2, :, :] = wide[0 : 2 * NDEV, :].astype(BF).reshape(NDEV, 2, 128)

    pl.semaphore_wait(barrier, 30)
    for k in range(1, 16):
        pl.semaphore_signal(ready, inc=1, device_id=at(ring, plane ^ k), device_id_type=MESH)

    def rest(step, carry):
        make(step)
        return carry

    def start(half, where):
        f, t = where
        pltpu.make_async_remote_copy(
            src_ref=sent.at[t * GROUPS + f, pl.ds(0, 3 - half)], dst_ref=got.at[me, pl.ds(0, 3 - half)],
            send_sem=send_sem.at[0], recv_sem=recv_sem.at[half], device_id=where, device_id_type=MESH,
        ).start()

    for half in range(2):

        @pl.when(tm == half)
        def _():
            def known(k, carry):
                start(half, at(ring ^ k, plane))
                start(half, at(ring, plane ^ k))
                return carry

            lax.fori_loop(1, 16, known, 0, unroll=5)

    lax.fori_loop(0, EARLY, rest, 0)
    pl.semaphore_wait(ready, 15)
    for half in range(2):

        @pl.when(tm == half)
        def _():
            def far(k, carry):
                for n in range(1, 16):
                    start(half, at(ring ^ k, plane ^ n))
                return carry

            lax.fori_loop(1, 16, far, 0)

    own = [
        pltpu.make_async_copy(sent.at[me], got.at[me], recv_sem.at[0]),
        pltpu.make_async_copy(sent.at[me, pl.ds(0, 2)], got.at[me, pl.ds(0, 2)], recv_sem.at[1]),
    ]
    for t in range(2):
        pl.when(tm == t)(own[t].start)

    lax.fori_loop(EARLY, 32, rest, 0)

    def whole(count, t):
        size = 3 - t
        return pltpu.make_async_remote_copy(
            src_ref=sent.at[pl.ds(0, count), pl.ds(0, size)], dst_ref=got.at[pl.ds(0, count), pl.ds(0, size)],
            send_sem=send_sem.at[0], recv_sem=recv_sem.at[t], device_id=(feed, tm), device_id_type=MESH,
        )

    for t in range(2):
        whole(GROUPS, t).wait_recv()
        for par in range(2):
            here = slice(t * GROUPS, t * GROUPS + GROUPS)
            wide[par * 256 : par * 256 + 256, :] = got[here, par].astype(F32).reshape(256, 128)
            for ri in range(2):
                block = wide[pl.ds(par * 256 + ri, 128, stride=2), :]
                turned[par, (ri * 2 + t) * 128 : (ri * 2 + t) * 128 + 128, :] = block.T
    wide[0:256, :] = got[0:GROUPS, 2].astype(F32).reshape(256, 128)
    block = wide[pl.ds(0, 128, stride=2), :].T
    for par in range(2):
        for ri in range(2):
            turned[par, (ri * 2 + 1) * 128 + 96 : (ri * 2 + 1) * 128 + 112, :] = block[(par * 2 + ri) * 16 : (par * 2 + ri) * 16 + 16]
        for i in range(16):
            lhs[par, :, i * 128 : i * 128 + 128] = turned[par, pl.ds(i, 32, stride=16), :].astype(BF)

    pairs[...] = jnp.zeros_like(pairs)
    scale = 1.0 / math.sqrt(FEEDS)
    lane = lax.broadcasted_iota(jnp.int32, (32, 128), 1) // 32

    unit = lax.broadcasted_iota(jnp.int32, (8, 128), 0)

    def whole_frames(x):
        first, second = x[:8], x[8:]
        terms = jnp.where(unit == 2, pltpu.roll(second, 4, 0), pltpu.roll(first, 2, 0))
        return first * scale, (second + jnp.where(unit < 3, terms, 0.0)) * scale

    def part(step):
        return (feed // 32 + jnp.where(step == 2, 3, jnp.where(step == 3, 2, step))) & 3

    def chunk(q):
        parts = []
        for par in range(2):
            both = jnp.concatenate([weights[par, q, 0], weights[par, q, 1]], axis=1)
            prod = jnp.dot(lhs[par], both, preferred_element_type=F32)
            real = prod[:16, :128] - prod[16:, 128:]
            imag = prod[:16, 128:] + prod[16:, :128]
            parts.append((whole_frames(real), whole_frames(imag)))
        rows = [parts[par][ri][t] for t in range(2) for par in range(2) for ri in range(2)]
        flip[...] = jnp.concatenate(rows + [jnp.zeros((64, 128), F32)], axis=0).T
        for t in range(2):
            acc = None
            for b in range(4):
                moved = flip[pl.ds(b, 32, stride=4), :]
                if b != t:
                    moved = pltpu.roll(moved, (32 * (b - t)) % 128, 1)
                acc = moved if acc is None else jnp.where(lane == b, moved, acc)
            pairs[pl.ds(0, 32, stride=2), :] = acc
            packed[pl.ds(t * GROUPS + q * 32, 32)] = pairs[...].astype(BF).reshape(32, 2, 128)

    def send(q, n):
        v = (n + feed) & 63
        t, f = v >> 5, q * 32 + (v & 31)
        to = t * GROUPS + f

        @pl.when(to != me)
        def _():
            pltpu.make_async_remote_copy(
                src_ref=packed.at[to], dst_ref=back_ref.at[me],
                send_sem=send_sem.at[1], recv_sem=recv_sem.at[2], device_id=(f, t), device_id_type=MESH,
            ).start()

    def later(step, carry):
        for n in range(64):
            send(part(step - 1), n)
        chunk(part(step))
        return carry

    def last(n, carry):
        send(part(jnp.int32(3)), n)
        return carry

    chunk(part(jnp.int32(0)))
    lax.fori_loop(1, 4, later, 0)
    lax.fori_loop(0, 64, last, 0, unroll=16)
    back_ref[me] = packed[me]
    pos_ids = lax.broadcasted_iota(jnp.int32, (8, 256), 1)
    for par in range(2):
        pos = (2 * pos_ids + par).astype(F32) * (1.0 / NCHAN)
        for b in range(4):
            chirp[par, b, 0], chirp[par, b, 1] = cos_sin((0.5 * rate_ref[b]) * (pos * pos))
    loads[6].wait()
    pltpu.make_async_remote_copy(
        src_ref=packed.at[pl.ds(0, NDEV - 1)], dst_ref=back_ref.at[pl.ds(0, NDEV - 1)],
        send_sem=send_sem.at[1], recv_sem=recv_sem.at[2], device_id=(feed, tm), device_id_type=MESH,
    ).wait()

    for t in range(2):
        pl.when(tm == t)(whole(NDEV - 1, t).wait_send)
    wide[...] = back_ref[...].astype(F32).reshape(2 * NDEV, 128)
    for h in range(2):
        turned[1, h * 128 : h * 128 + 128, :] = wide[pl.ds(h * 256, 128, stride=2), :].T
    halves = []
    for par in range(2):
        real, imag = [], []
        for b in range(4):
            spot = b * 32 + par * 16
            xr, xi = [
                jnp.concatenate([turned[1, h * 128 + spot + o : h * 128 + spot + o + 8, :] for h in range(2)], axis=1)
                for o in (0, 8)
            ]
            c, sn = chirp[par, b, 0], chirp[par, b, 1]
            real.append(xr * c - xi * sn)
            imag.append(xr * sn + xi * c)
        hi, lo = split(jnp.concatenate(real + imag, axis=0))
        top = inverse[0, par]
        prod = (
            jnp.dot(hi, top, preferred_element_type=F32)
            + jnp.dot(lo, top, preferred_element_type=F32)
            + jnp.dot(hi, inverse[1, par], preferred_element_type=F32)
        )
        halves.append((prod[:32, :256] - prod[32:, 256:], prod[:32, 256:] + prod[32:, :256]))
    (er, ei), (sr, si) = halves
    for b in range(4):
        rows = slice(b * 8, b * 8 + 6)
        o_ref[:, b, 0:256] = er[rows] + sr[rows]
        o_ref[:, b, 256:512] = er[rows] - sr[rows]
        o_ref[:, b, 512:768] = ei[rows] + si[rows]
        o_ref[:, b, 768:1024] = ei[rows] - si[rows]


def body(samples, filter_taps, feed_cylinder, feed_delay, pointing, chirp_rate):
    series = pl.pallas_call(
        main_kernel,
        out_shape=jax.ShapeDtypeStruct((6, 4, 2 * NCHAN), F32),
        in_specs=[pl.BlockSpec(memory_space=pl.ANY)] * 7 + [pl.BlockSpec(memory_space=pltpu.SMEM)], out_specs=VMEM,
        scratch_shapes=[
            pltpu.VMEM((16, 6 * 2 * NCHAN), BF),
            pltpu.VMEM((TAPS, 2 * NCHAN), F32),
            pltpu.VMEM((16, 128), jnp.int32),
            pltpu.VMEM((16, 128), jnp.int32),
            pltpu.VMEM((CYL, BEAMS), jnp.int32),
            pltpu.VMEM((2, 2, NCHAN, NCHAN), BF),
            pltpu.VMEM((2, 144, NCHAN), F32),
            pltpu.VMEM((NDEV, 3, 2, 128), BF),
            pltpu.VMEM((NDEV, 3, 2, 128), BF),
            pltpu.VMEM((2, 4, 2, FEEDS, 128), BF),
            pltpu.VMEM((3, GROUPS, 128), F32),
            pltpu.VMEM((4, 8, 128), F32),
            pltpu.VMEM((2 * NDEV, 128), F32),
            pltpu.VMEM((2, 512, 128), F32),
            pltpu.VMEM((2, 32, FEEDS), BF),
            pltpu.VMEM((128, 128), F32),
            pltpu.VMEM((64, 128), F32),
            pltpu.VMEM((NDEV, 2, 128), BF),
            pltpu.VMEM((NDEV, 2, 128), BF),
            pltpu.VMEM((2, 2, NCHAN // 2, NCHAN), BF),
            pltpu.VMEM((2, 4, 2, 8, 256), F32),
            pltpu.SemaphoreType.DMA((7,)),
            pltpu.SemaphoreType.REGULAR,
            pltpu.SemaphoreType.DMA((2,)),
            pltpu.SemaphoreType.DMA((3,)),
        ],
        compiler_params=pltpu.CompilerParams(collective_id=0, has_side_effects=True, vmem_limit_bytes=MAIN_VMEM),
    )(samples, filter_taps, feed_delay.reshape(16, 128), feed_cylinder.reshape(16, 128), pointing.T, jnp.asarray(forward_rows()), jnp.asarray(inverse_rows()), chirp_rate)
    return jnp.transpose(series, (1, 0, 2))


def solution(mesh):
    return jax.shard_map(
        body,
        mesh=mesh,
        in_specs=(P("feed", "tm"), P(), P(), P(), P(), P("feed")),
        out_specs=P("feed", "tm", None),
        check_vma=False,
    )
```
